32 devices in a mesh: row: 8 (over y, x, core), col: 4 (over z).
Axes of the slice: x: 2, y: 2, z: 4, core: 2. Of those that a mesh axis runs over, the one named last changes fastest.
Arguments:
- snapshots: float32 [16384, 2048], P(('row', 'col')), may hold values from -6 to 6
- district: int32 [16384], P(('row', 'col')), may hold values from 0 to 63, never falling along the last dimension, each value on 1 to 1024 neighbouring positions
- target: int32 [16384], replicated, may hold values from 0 to 16383, as said below
Outputs:
- coefficients: float32 [512, 2048], P(None, 'col')
- remainder: float32 [16384, 2048], P('row', 'col')
The draws below stay inside these ranges and needn't reach their ends.
Inputs may be any that keep to these rules, and one draw needn't show every extreme that they name: A permutation of the storage rows; each aligned block of 512 nodes has exactly 512 / 8 nodes whose target lies in each aligned block of 2048 storage rows. `district`: districts never fall along the nodes, and each holds at most 1024 nodes.
All inputs are finite; a program needn't handle non-finite values.
Results may differ from the reference program's by a relative error of at most 0.0001.
Values sent between devices are 32-bit elements; how exact they have to be, the bound alone decides.
No kernel may reach another device: no remote copies, remote signals or barrier semaphores. Data moves between devices by JAX's collectives and lax.ppermute only.
A program may use at most 128 MiB of HBM per device.

```python
import math
import jax
import jax.numpy as jnp
import numpy as np
from jax import lax

NODES_DEV = 512
SNAPS = 2048
NB = 256
DIST_MEAN = 256
NODES = 16384
NDIST = 64
LOC = 2048
SOURCES = 32
N_COL = 4


def draw_target(key, part):
    first_key, second_key = jax.random.split(key)
    owners = NODES // LOC
    per_owner = NODES_DEV // owners
    owner_keys = jax.random.split(first_key, owners)
    slots = jax.vmap(lambda single: jax.random.permutation(single, LOC))(owner_keys)
    slots = slots.reshape(owners, SOURCES, per_owner)
    placed = jnp.arange(owners, dtype=jnp.int32)[:, None, None] * LOC + slots.astype(jnp.int32)
    by_source = placed.transpose(1, 0, 2).reshape(SOURCES, NODES_DEV)
    source_keys = jax.random.split(second_key, SOURCES)
    shuffle = jax.vmap(lambda single: jax.random.permutation(single, NODES_DEV))(source_keys)
    result = jnp.take_along_axis(by_source, shuffle.astype(jnp.int32), axis=1)
    return result.reshape(NODES).astype(jnp.int32)


def block_levels(own_key, dims, cuts, smallest, largest):
    def one(position, blocks):
        steps = jax.random.uniform(jax.random.fold_in(jax.random.fold_in(own_key, 6), position), (blocks,), jnp.float32, smallest / len(cuts), largest / len(cuts))
        return jnp.repeat(jnp.exp(steps), dims[position] // blocks).reshape((-1,) + (1,) * (len(dims) - position - 1))

    gain = one(*cuts[0])
    for cut in cuts[1:]:
        gain = gain * one(*cut)
    return gain


def length_profile(number_of, total, bound, slope):
    weights = [(1 << 20) // math.isqrt(standing ** slope) + 1 for standing in range(2, number_of + 1)]
    rest, given = total - bound - (number_of - 1), [1] * (number_of - 1)
    while rest > 0:
        candidates = [i for i in range(number_of - 1) if given[i] < bound]
        pool, remaining = sum([weights[i] for i in candidates]), rest
        for i in candidates:
            more = min(bound - given[i], max(1, remaining * weights[i] // pool), rest)
            given[i] = given[i] + more
            rest = rest - more
    return np.array([bound] + given)


def uneven_parts(own_key, number_of, total, most, slope):
    if number_of == 2:
        one = jax.random.randint(own_key, (), max(1, total - most), min(most, total - 1) + 1)
        return jnp.stack([one, total - one])
    sizes = jnp.asarray(length_profile(number_of, total, most, slope), jnp.int32)
    couples = (number_of - 1) // 2
    giver, receiver = sizes[1:1 + 2 * couples:2], sizes[2:2 + 2 * couples:2]
    room = jnp.minimum(giver - 1, most - receiver)
    shifted = jax.random.randint(jax.random.fold_in(own_key, 1), (couples,), 0, 1 << 20) % (room + 1)
    sizes = sizes.at[1:1 + 2 * couples:2].set(giver - shifted).at[2:2 + 2 * couples:2].set(receiver + shifted)
    return sizes[jax.random.permutation(jax.random.fold_in(own_key, 2), number_of)]


def bell_draw(own_key, extent, scale, limit, shards=(), kind=jnp.bfloat16):
    drawn = scale * jax.random.normal(own_key, extent, jnp.float32)
    if shards:
        drawn = drawn * block_levels(own_key, extent, shards, -0.22, 0.18)
    return jnp.clip(drawn, -limit, limit).astype(kind)


def setup_inputs(seed: int = 0) -> dict:
    splits = jax.random.split(jax.random.key(seed), 4)
    snapshots = bell_draw(splits[0], (NODES, SNAPS), 1.0, 6.0, ((0, 32),), jnp.float32)
    district = jnp.searchsorted(jnp.cumsum(uneven_parts(splits[1], NDIST, NODES, 4 * DIST_MEAN, 2)), jnp.arange(NODES), side="right").astype(jnp.int32)
    target = draw_target(jax.random.fold_in(splits[3], 71), 0)
    return dict(snapshots=snapshots, district=district, target=target)


HIGH = lax.Precision.HIGHEST

def orthonormal(panel, gram):
    lower = jnp.linalg.cholesky(gram)
    inverse = jax.scipy.linalg.solve_triangular(lower, jnp.eye(gram.shape[0], dtype=gram.dtype), lower=True)
    return jnp.dot(panel, inverse.T, precision=HIGH)

def reference(snapshots, district, target):
    nodes = snapshots.shape[0]
    counts = jax.ops.segment_sum(jnp.ones((nodes,), jnp.float32), district, num_segments=NDIST)
    scale = jnp.sqrt(DIST_MEAN / jnp.maximum(counts, 1.0))
    weighted = snapshots * scale[district][:, None]
    grid = jnp.zeros((nodes, SNAPS), jnp.float32).at[target].set(weighted)
    grid = grid.reshape(nodes, SNAPS // (NB * N_COL), N_COL, NB).transpose(0, 2, 1, 3).reshape(nodes, SNAPS)
    stacked = []
    for panel_index in range(2):
        start = panel_index % N_COL * (SNAPS // N_COL) + panel_index // N_COL * NB
        panel = grid[:, start:start + NB]
        gram = jnp.dot(panel.T, panel, precision=HIGH)
        basis = orthonormal(panel, gram)
        projection = jnp.dot(basis.T, grid, precision=HIGH)
        grid = grid - jnp.dot(basis, projection, precision=HIGH)
        stacked.append(projection)
    return (jnp.concatenate(stacked, axis=0), grid)
```

```python
import functools

import jax
import jax.numpy as jnp
from jax import lax
from jax.experimental import pallas as pl
from jax.experimental.pallas import tpu as pltpu
from jax.sharding import PartitionSpec as P

NB = 256
DIST_MEAN = 256
DIST_MOST = 4 * DIST_MEAN
PANELS = 2
BLOCK = 128
GROUP = 8
HIGH = lax.Precision.HIGHEST


def matmul(a, b):
    return jnp.dot(a, b, precision=HIGH, preferred_element_type=jnp.float32)


def contract_rows(a, b):
    return lax.dot_general(
        a, b, (((0,), (0,)), ((), ())), precision=HIGH, preferred_element_type=jnp.float32
    )


def eliminate(block):
    tiles = [block[8 * t : 8 * t + 8] for t in range(BLOCK // 8)]
    sub = lax.broadcasted_iota(jnp.int32, (8, BLOCK), 0)
    lane = lax.broadcasted_iota(jnp.int32, (8, BLOCK), 1)
    inverse = [jnp.where(lane == sub + 8 * t, 1.0, 0.0) for t in range(BLOCK // 8)]

    def along(x, j):
        return jnp.broadcast_to(x[:, j : j + 1], (8, BLOCK))

    def down(x, r):
        return jnp.broadcast_to(x[r : r + 1, :], (8, BLOCK))

    for first in range(0, BLOCK, GROUP):
        t = first // 8
        own = [along(tiles[t], first + q) for q in range(GROUP)]
        below = {
            u: [along(tiles[u], first + q) for q in range(GROUP)]
            for u in range(t + 1, BLOCK // 8)
        }
        recips, rows, inverse_rows, cross = [], [], [], []
        for a in range(GROUP):
            r = first % 8 + a
            pivots = {q: down(own[q], r) for q in range(a, GROUP)}
            recip = 1.0 / pivots[a]
            factor = jnp.where(sub > r, own[a] * recip, 0.0)
            for q in range(a + 1, GROUP):
                own[q] = own[q] - factor * pivots[q]
            row, inverse_row = down(tiles[t], r), down(inverse[t], r)
            tiles[t] = tiles[t] - factor * row
            inverse[t] = inverse[t] - factor * inverse_row
            recips.append(recip)
            rows.append(row)
            inverse_rows.append(inverse_row)
            cross.append(pivots)
        for u in range(t + 1, BLOCK // 8):
            mine = below[u]
            for a in range(GROUP):
                factor = mine[a] * recips[a]
                for q in range(a + 1, GROUP):
                    mine[q] = mine[q] - factor * cross[a][q]
                tiles[u] = tiles[u] - factor * rows[a]
                inverse[u] = inverse[u] - factor * inverse_rows[a]
    out = []
    for t in range(BLOCK // 8):
        pivot = jnp.sum(jnp.where(lane == sub + 8 * t, tiles[t], 0.0), axis=1, keepdims=True)
        out.append(inverse[t] * (1.0 / jnp.sqrt(pivot)))
    return jnp.concatenate(out, axis=0)


def inverse_factor_kernel(gram_ref, out_ref, work):
    n = gram_ref.shape[0]
    work[:, :n] = gram_ref[...]
    down = lax.broadcasted_iota(jnp.int32, (n, n), 0)
    along = lax.broadcasted_iota(jnp.int32, (n, n), 1)
    work[:, n:] = jnp.where(down == along, 1.0, 0.0)
    column = lax.broadcasted_iota(jnp.int32, (BLOCK, n), 1)

    def step(k, carry):
        at = pl.multiple_of(k * BLOCK, BLOCK)
        inverse = eliminate(work[pl.ds(at, BLOCK), pl.ds(at, BLOCK)])
        rows = matmul(inverse, work[pl.ds(at, BLOCK), :])
        out_ref[pl.ds(at, BLOCK), :] = rows[:, n:]
        later = jnp.where(column >= at + BLOCK, rows[:, :n], 0.0)
        work[...] -= contract_rows(later, rows)
        return carry

    lax.fori_loop(0, n // BLOCK, step, 0)


def inverse_factor(gram):
    n = gram.shape[0]
    return pl.pallas_call(
        inverse_factor_kernel,
        out_shape=jax.ShapeDtypeStruct((n, n), jnp.float32),
        in_specs=[pl.BlockSpec(memory_space=pltpu.VMEM)],
        out_specs=pl.BlockSpec(memory_space=pltpu.VMEM),
        scratch_shapes=[pltpu.VMEM((n, 2 * n), jnp.float32)],
        cost_estimate=pl.CostEstimate(flops=6 * n**3, bytes_accessed=8 * n * n, transcendentals=0),
        name="inverse_factor",
    )(gram)


def shift_exchange(pieces, axis, group, index, count, stride):
    total = lax.dynamic_index_in_dim(pieces, index, 0, keepdims=False)
    for k in range(1, count):
        sent = lax.dynamic_index_in_dim(pieces, (index + k) % count, 0, keepdims=False)
        total = total + lax.ppermute(sent, axis, shift_pairs(group, count, stride, k))
    return total


def shift_pairs(size, count, stride, k):
    pairs = []
    for i in range(size):
        member = i // stride % count
        pairs.append((i, i + ((member + k) % count - member) * stride))
    return pairs


def shift_gather(piece, axis, group, index, count, stride):
    held = [piece] + [None] * (count - 1)
    for k in range(1, count):
        held[count - k] = lax.ppermute(piece, axis, shift_pairs(group, count, stride, k))
    twice = jnp.stack(held + held)
    return lax.dynamic_slice_in_dim(twice, (count - index) % count, count, 0)


def levels_of(n_row, n_col):
    row, col = lax.axis_index("row"), lax.axis_index("col")
    return (
        ("row", n_row, row % 2, 2, 1),
        ("row", n_row, row // 2, n_row // 2, 2),
        ("col", n_col, col, n_col, 1),
    )


def all_sum(value, levels):
    shapes = []
    for level in levels:
        count = level[3]
        shapes.append(value.shape)
        pieces = value.reshape(count, value.shape[0] // count, *value.shape[1:])
        value = shift_exchange(pieces, *level)
    for level, shape in zip(reversed(levels), reversed(shapes)):
        value = shift_gather(value, *level).reshape(shape)
    return value


def place_kernel(place_ref, rows_ref, out_ref):
    def step(k, carry):
        out_ref[pl.ds(place_ref[k], 1), :] = rows_ref[pl.ds(k, 1), :]
        return carry

    lax.fori_loop(0, rows_ref.shape[0], step, 0, unroll=8)


def place_rows(rows, place):
    return pl.pallas_call(
        place_kernel,
        out_shape=jax.ShapeDtypeStruct(rows.shape, rows.dtype),
        in_specs=[
            pl.BlockSpec(memory_space=pltpu.SMEM),
            pl.BlockSpec(memory_space=pltpu.VMEM),
        ],
        out_specs=pl.BlockSpec(memory_space=pltpu.VMEM),
        cost_estimate=pl.CostEstimate(flops=0, bytes_accessed=8 * rows.size, transcendentals=0),
        name="place_rows",
    )(place, rows)


def count_before(mask):
    n = mask.shape[-1]
    before = (jnp.arange(n)[:, None] < jnp.arange(n)[None, :]).astype(jnp.bfloat16)
    counts = jnp.dot(mask.astype(jnp.bfloat16), before, preferred_element_type=jnp.float32)
    return counts.astype(jnp.int32)


def body(snapshots, district, target):
    n_row, n_col = lax.axis_size("row"), lax.axis_size("col")
    row, col = lax.axis_index("row"), lax.axis_index("col")
    nodes_dev, snaps = snapshots.shape
    nodes = target.shape[0]
    groups = nodes // DIST_MEAN
    local_rows = nodes // n_row
    per_owner = nodes_dev // n_row
    width = snaps // n_col
    sources = n_row * n_col

    labels = jnp.arange(groups, dtype=jnp.int32)
    member = district[:, None] == labels[None, :]
    own = jnp.sum(member.astype(jnp.float32), axis=0)
    counts = own
    reach = -(-(DIST_MOST - 1) // nodes_dev)
    for k in range(1, reach + 1):
        up = [(i, i + k) for i in range(sources - k)]
        down = [(i + k, i) for i in range(sources - k)]
        counts = counts + lax.ppermute(own, ("row", "col"), up)
        counts = counts + lax.ppermute(own, ("row", "col"), down)
    scale = jnp.sqrt(DIST_MEAN / jnp.maximum(counts, 1.0))
    weight = jnp.sum(jnp.where(member, scale[None, :], 0.0), axis=1)
    weighted = snapshots * weight[:, None]

    panel = weighted[:, : PANELS * NB]
    levels = levels_of(n_row, n_col)
    gram = all_sum(contract_rows(panel, panel), levels)
    cross = all_sum(contract_rows(panel, weighted[:, PANELS * NB :]), levels)
    inverse = inverse_factor(gram)
    cross = jnp.concatenate([gram, cross], axis=1)
    cross = cross.reshape(PANELS * NB, width // NB, n_col, NB)
    basis = lax.dot_general(
        panel, inverse, (((1,), (1,)), ((), ())), precision=HIGH, preferred_element_type=jnp.float32
    )
    split = weighted.reshape(nodes_dev, width // NB, n_col, NB)

    def part(of, block):
        taken = lax.dynamic_index_in_dim(of, block, 2, keepdims=False)
        return taken.reshape(of.shape[0], width)

    owner = target.reshape(sources, nodes_dev) // local_rows
    at_me = owner == row
    rank = count_before(at_me)
    slots = jnp.arange(per_owner, dtype=jnp.int32)
    chosen = at_me[:, None, :] & (rank[:, None, :] == slots[None, :, None])
    local = target.reshape(sources, nodes_dev) - row * local_rows
    place = jnp.sum(jnp.where(chosen, local[:, None, :], 0), axis=2)
    place = place.reshape(n_row, n_col, per_owner)

    def order_of(plane):
        there = lax.dynamic_index_in_dim(owner, row * n_col + plane, 0, keepdims=False)
        to = there[None, :] == jnp.arange(n_row, dtype=jnp.int32)[:, None]
        place_in = count_before(to)
        hit = to[:, None, :] & (place_in[:, None, :] == slots[None, :, None])
        index = jnp.arange(nodes_dev, dtype=jnp.int32)
        return jnp.sum(jnp.where(hit, index, 0), axis=2).reshape(nodes_dev)

    own_cross = matmul(inverse, part(cross, col))
    arrived, places = [], []
    for k in range(n_col):
        to = (col + k) % n_col
        factor = own_cross if k == 0 else matmul(inverse, part(cross, to))
        rest = part(split, to) - matmul(basis, factor)
        plane = (col - k) % n_col
        if k > 0:
            rest = lax.ppermute(rest, "col", shift_pairs(n_col, n_col, 1, k))
        rest = rest[order_of(plane)]
        arrived.append(lax.all_to_all(rest, "row", split_axis=0, concat_axis=0, tiled=True))
        places.append(
            lax.dynamic_index_in_dim(place, plane, 1, keepdims=False).reshape(nodes_dev)
        )
    remainder = place_rows(jnp.concatenate(arrived), jnp.concatenate(places))
    return (own_cross, remainder)


def solution(mesh):
    in_specs = (P(("row", "col"), None), P(("row", "col")), P())
    out_specs = (P(None, "col"), P("row", "col"))
    return jax.shard_map(body, mesh=mesh, in_specs=in_specs, out_specs=out_specs, check_vma=False)
```

```python
import functools

import jax
import jax.numpy as jnp
from jax import lax
from jax.experimental import pallas as pl
from jax.experimental.pallas import tpu as pltpu
from jax.sharding import PartitionSpec as P


NB = 256
DIST_MEAN = 256
PANELS = 2
BLOCK = 128
GROUP = 8
HIGH = lax.Precision.HIGHEST


def matmul(a, b):
    return jnp.dot(a, b, precision=HIGH, preferred_element_type=jnp.float32)


def contract_rows(a, b):
    return lax.dot_general(
        a, b, (((0,), (0,)), ((), ())), precision=HIGH, preferred_element_type=jnp.float32
    )


def eliminate(block):
    tiles = [block[8 * t : 8 * t + 8] for t in range(BLOCK // 8)]
    sub = lax.broadcasted_iota(jnp.int32, (8, BLOCK), 0)
    lane = lax.broadcasted_iota(jnp.int32, (8, BLOCK), 1)
    inverse = [jnp.where(lane == sub + 8 * t, 1.0, 0.0) for t in range(BLOCK // 8)]

    def along(x, j):
        return jnp.broadcast_to(x[:, j : j + 1], (8, BLOCK))

    def down(x, r):
        return jnp.broadcast_to(x[r : r + 1, :], (8, BLOCK))

    for first in range(0, BLOCK, GROUP):
        t = first // 8
        own = [along(tiles[t], first + q) for q in range(GROUP)]
        below = {
            u: [along(tiles[u], first + q) for q in range(GROUP)]
            for u in range(t + 1, BLOCK // 8)
        }
        recips, rows, inverse_rows, cross = [], [], [], []
        for a in range(GROUP):
            r = first % 8 + a
            pivots = {q: down(own[q], r) for q in range(a, GROUP)}
            recip = 1.0 / pivots[a]
            factor = jnp.where(sub > r, own[a] * recip, 0.0)
            for q in range(a + 1, GROUP):
                own[q] = own[q] - factor * pivots[q]
            row, inverse_row = down(tiles[t], r), down(inverse[t], r)
            tiles[t] = tiles[t] - factor * row
            inverse[t] = inverse[t] - factor * inverse_row
            recips.append(recip)
            rows.append(row)
            inverse_rows.append(inverse_row)
            cross.append(pivots)
        for u in range(t + 1, BLOCK // 8):
            mine = below[u]
            for a in range(GROUP):
                factor = mine[a] * recips[a]
                for q in range(a + 1, GROUP):
                    mine[q] = mine[q] - factor * cross[a][q]
                tiles[u] = tiles[u] - factor * rows[a]
                inverse[u] = inverse[u] - factor * inverse_rows[a]
    out = []
    for t in range(BLOCK // 8):
        pivot = jnp.sum(jnp.where(lane == sub + 8 * t, tiles[t], 0.0), axis=1, keepdims=True)
        out.append(inverse[t] * (1.0 / jnp.sqrt(pivot)))
    return jnp.concatenate(out, axis=0)


def factor_step(k, work, out_ref):
    n = out_ref.shape[0]
    column = lax.broadcasted_iota(jnp.int32, (BLOCK, n), 1)
    at = pl.multiple_of(k * BLOCK, BLOCK)
    inverse = eliminate(work[pl.ds(at, BLOCK), pl.ds(at, BLOCK)])
    rows = matmul(inverse, work[pl.ds(at, BLOCK), :])
    out_ref[pl.ds(at, BLOCK), :] = rows[:, n:]
    later = jnp.where(column >= at + BLOCK, rows[:, :n], 0.0)
    work[...] -= contract_rows(later, rows)


def first_half_kernel(gram_ref, out_ref, work):
    n = gram_ref.shape[0]
    work[:, :n] = gram_ref[...]
    down = lax.broadcasted_iota(jnp.int32, (n, n), 0)
    along = lax.broadcasted_iota(jnp.int32, (n, n), 1)
    work[:, n:] = jnp.where(down == along, 1.0, 0.0)
    out_ref[...] = jnp.zeros((n, n), jnp.float32)

    def step(k, carry):
        factor_step(k, work, out_ref)
        return carry

    lax.fori_loop(0, n // BLOCK // 2, step, 0)


def second_half_kernel(held_ref, work_ref, out_ref, work):
    n = out_ref.shape[0]
    out_ref[...] = held_ref[...]
    work[...] = work_ref[...]

    def step(k, carry):
        factor_step(k, work, out_ref)
        return carry

    lax.fori_loop(n // BLOCK // 2, n // BLOCK, step, 0)


def inverse_factor(gram):
    n = gram.shape[0]
    vmem = pl.BlockSpec(memory_space=pltpu.VMEM)
    cost = pl.CostEstimate(flops=3 * n**3, bytes_accessed=8 * n * n, transcendentals=0)
    inverse = jax.ShapeDtypeStruct((n, n), jnp.float32)
    work = jax.ShapeDtypeStruct((n, 2 * n), jnp.float32)
    held, left = pl.pallas_call(
        first_half_kernel,
        out_shape=(inverse, work),
        in_specs=[vmem],
        out_specs=(vmem, vmem),
        cost_estimate=cost,
        name="first_half",
    )(gram)
    return pl.pallas_call(
        second_half_kernel,
        out_shape=inverse,
        in_specs=[vmem, vmem],
        out_specs=vmem,
        scratch_shapes=[pltpu.VMEM((n, 2 * n), jnp.float32)],
        cost_estimate=cost,
        name="second_half",
    )(held, left)


def spread(value, axes, count):
    copies = jnp.broadcast_to(value[None], (count, *value.shape))
    return lax.all_to_all(copies, axes, split_axis=0, concat_axis=0, tiled=True)


def scatter_sum(pieces, axes):
    pieces = lax.all_to_all(pieces, axes, split_axis=0, concat_axis=0, tiled=True)
    return jnp.sum(pieces, axis=0)


def swap_pairs(size, k):
    return [(i, i ^ k) for i in range(size)]


def column_sum(value, n_col):
    bit = 1
    while bit < n_col:
        value = value + lax.ppermute(value, "col", swap_pairs(n_col, bit))
        bit *= 2
    return value


def row_scatter_sum(pieces, n_row, row):
    half, odd = n_row // 2, row % 2
    pairs = pieces.reshape(half, 2, *pieces.shape[1:])
    other = lax.ppermute(
        lax.dynamic_index_in_dim(pairs, 1 - odd, 1, keepdims=False),
        "row",
        [(i, i ^ 1) for i in range(n_row)],
    )
    kept = lax.dynamic_index_in_dim(pairs, odd, 1, keepdims=False) + other
    place = row // 2
    total = lax.dynamic_index_in_dim(kept, place, 0, keepdims=False)
    arrived = []
    for k in range(1, half):
        arrived.append(
            lax.ppermute(
                lax.dynamic_index_in_dim(kept, (place + k) % half, 0, keepdims=False),
                "row",
                [(i, (i // 2 + k) % half * 2 + i % 2) for i in range(n_row)],
            )
        )
    for piece in arrived:
        total = total + piece
    return total


def col_scatter_sum(pieces, extra, n_col, col):
    rows = pieces.shape[1]
    total = lax.dynamic_index_in_dim(pieces, col, 0, keepdims=False)
    extras = [extra]
    for k in range(1, n_col):
        sent = lax.dynamic_index_in_dim(pieces, col ^ k, 0, keepdims=False)
        got = lax.ppermute(jnp.concatenate([sent, extra]), "col", swap_pairs(n_col, k))
        total = total + got[:rows]
        extras.append(got[rows:])
    return total, extras


def relay(value, n_col, up):
    held = [value]
    for t in range(1, n_col):
        if up:
            pairs = [(i, i + 1) for i in range(t - 1, n_col - 1)]
        else:
            pairs = [(i, i - 1) for i in range(1, n_col - t + 1)]
        held.append(lax.ppermute(held[-1], "col", pairs))
    return held


def correct_kernel(slot_ref, choice_ref, rows_ref, weight_ref, factor_ref, *rest):
    *panel_refs, out_ref, scratch = rest
    panel = panel_refs[0][...]
    for index, ref in enumerate(panel_refs[1:]):
        panel = jnp.where(choice_ref[0] == index + 1, ref[...], panel)
    scratch[...] = (rows_ref[...] - matmul(panel, factor_ref[...])) * weight_ref[...]

    def step(k, carry):
        out_ref[pl.ds(slot_ref[k], 1), :] = scratch[pl.ds(k, 1), :]
        return carry

    lax.fori_loop(0, rows_ref.shape[0], step, 0, unroll=8)


def correct(slot, choice, rows, weight, factor, panels):
    inner = factor.shape[0]
    smem, vmem = (pl.BlockSpec(memory_space=space) for space in (pltpu.SMEM, pltpu.VMEM))
    return pl.pallas_call(
        correct_kernel,
        out_shape=jax.ShapeDtypeStruct(rows.shape, rows.dtype),
        in_specs=[smem] * 2 + [vmem] * (3 + len(panels)),
        out_specs=vmem,
        scratch_shapes=[pltpu.VMEM(rows.shape, rows.dtype)],
        cost_estimate=pl.CostEstimate(
            flops=12 * rows.size * inner, bytes_accessed=16 * rows.size, transcendentals=0
        ),
        name="correct",
    )(slot, choice.reshape(1), rows, weight, factor, *panels)


def place_kernel(held, place_ref, *rest):
    *rows_refs, out_ref = rest
    if held:
        *rows_refs, held_ref = rows_refs
        out_ref[...] = held_ref[...]
    for index, rows_ref in enumerate(rows_refs):

        def step(k, carry, index=index, rows_ref=rows_ref):
            out_ref[pl.ds(place_ref[index, k], 1), :] = rows_ref[pl.ds(k, 1), :]
            return carry

        lax.fori_loop(0, rows_ref.shape[0], step, 0, unroll=8)


def place_rows(chunks, place, shape, held=None):
    vmem = pl.BlockSpec(memory_space=pltpu.VMEM)
    operands = list(chunks) + ([] if held is None else [held])
    return pl.pallas_call(
        functools.partial(place_kernel, held is not None),
        out_shape=jax.ShapeDtypeStruct(shape, chunks[0].dtype),
        in_specs=[pl.BlockSpec(memory_space=pltpu.SMEM)] + [vmem] * len(operands),
        out_specs=vmem,
        input_output_aliases={} if held is None else {len(operands): 0},
        cost_estimate=pl.CostEstimate(
            flops=0, bytes_accessed=8 * sum(c.size for c in chunks), transcendentals=0
        ),
        name="place_rows",
    )(place, *operands)


def count_before(mask):
    n = mask.shape[-1]
    before = (jnp.arange(n)[:, None] < jnp.arange(n)[None, :]).astype(jnp.bfloat16)
    counts = jnp.dot(mask.astype(jnp.bfloat16), before, preferred_element_type=jnp.float32)
    return counts.astype(jnp.int32)


def slots_of(owner, n_row, per_owner):
    blocks, nodes = owner.shape
    to = owner[:, None, :] == jnp.arange(n_row, dtype=jnp.int32)[None, :, None]
    before = count_before(to.reshape(blocks * n_row, nodes)).reshape(to.shape)
    rank = jnp.sum(jnp.where(to, before, 0), axis=1)
    return owner * per_owner + rank


def places_of(owner, target, row, local_rows, per_owner):
    mine = owner == row
    rank = jnp.where(mine, count_before(mine), -1)
    hit = rank[:, None, :] == jnp.arange(per_owner, dtype=jnp.int32)[None, :, None]
    local = jnp.where(mine, target - row * local_rows, 0)
    digits = jnp.stack([local // 256, local % 256], axis=1).astype(jnp.bfloat16)
    found = lax.dot_general(
        digits,
        hit.astype(jnp.bfloat16),
        (((2,), (2,)), ((0,), (0,))),
        preferred_element_type=jnp.float32,
    ).astype(jnp.int32)
    return found[:, 0] * 256 + found[:, 1]


def steps(snapshots, district, target):
    n_row, n_col = lax.axis_size("row"), lax.axis_size("col")
    row, col = lax.axis_index("row"), lax.axis_index("col")
    nodes_dev, snaps = snapshots.shape
    nodes = target.shape[0]
    groups = nodes // DIST_MEAN
    local_rows = nodes // n_row
    per_owner = nodes_dev // n_row
    width = snaps // n_col
    sources = n_row * n_col
    inner = PANELS * NB

    def part(block):
      taken = [
          lax.dynamic_slice_in_dim(snapshots, (group * n_col + block) * NB, NB, axis=1)
          for group in range(width // NB)
      ]
      return jnp.concatenate(taken, axis=1)

    panel = snapshots[:, :inner]
    panel_sent = lax.optimization_barrier(snapshots)[:, :inner]
    rows = [part(col)]
    for k in range(1, n_col):
        sent = part(col ^ k)
        rows.append(lax.ppermute(sent, "col", swap_pairs(n_col, k)))
    below, above = relay(panel_sent, n_col, True), relay(panel_sent, n_col, False)

    labels = jnp.arange(groups, dtype=jnp.int32)
    member = district[:, None] == labels[None, :]
    own = jnp.sum(member.astype(jnp.float32), axis=0)
    counts = spread(own, ("row", "col"), sources)
    counts = jnp.sum(counts, axis=0)
    square = DIST_MEAN / jnp.maximum(counts, 1.0)
    root = jnp.sqrt(square)
    weight = jnp.sum(jnp.where(member, root[None, :], 0.0), axis=1, keepdims=True)
    squares = jnp.sum(jnp.where(member, square[None, :], 0.0), axis=1, keepdims=True)

    heavy = panel * squares
    gram = contract_rows(heavy, panel).reshape(n_row, inner // n_row, inner)
    own_gram = scatter_sum(gram, "row")
    gram = column_sum(own_gram, n_col)
    gram = spread(gram, "row", n_row).reshape(inner, inner)

    cross = contract_rows(heavy, snapshots[:, inner:])
    cross = row_scatter_sum(cross.reshape(n_row, inner // n_row, snaps - inner), n_row, row)
    cross = jnp.concatenate([own_gram, cross], axis=1)
    cross = cross.reshape(inner // n_row, width // NB, n_col, NB).transpose(2, 0, 1, 3)
    cross, weights = col_scatter_sum(
        cross.reshape(n_col, inner // n_row, width), weight.reshape(-1, width), n_col, col
    )
    cross = spread(cross, "row", n_row).reshape(inner, width)

    inverse = inverse_factor(gram)
    coefficients = matmul(inverse, cross)
    factor = contract_rows(inverse, coefficients)

    owner = target.reshape(sources, nodes_dev) // local_rows
    place = places_of(owner, target.reshape(sources, nodes_dev), row, local_rows, per_owner)
    place = place.reshape(n_row, n_col, per_owner)
    slot = slots_of(lax.dynamic_slice_in_dim(owner, row * n_col, n_col), n_row, per_owner)

    chunks, places = [], []
    for k in range(n_col):
        plane = col ^ k
        panels, choice = [panel_sent], jnp.int32(0)
        if k > 0:
            steps_to = sorted({(i ^ k) - i for i in range(n_col)})
            panels = [below[-d] if d < 0 else above[d] for d in steps_to]
            for index, d in enumerate(steps_to):
                choice = jnp.where(plane - col == d, index, choice)
        chunk = correct(
            lax.dynamic_index_in_dim(slot, plane, 0, keepdims=False),
            choice,
            rows[k],
            weights[k].reshape(nodes_dev, 1),
            factor,
            panels,
        )
        chunks.append(lax.all_to_all(chunk, "row", split_axis=0, concat_axis=0, tiled=True))
        places.append(
            lax.dynamic_index_in_dim(place, plane, 1, keepdims=False).reshape(nodes_dev)
        )
    shape = (local_rows, width)
    remainder = place_rows(chunks[:-1], jnp.stack(places[:-1]), shape)
    remainder = place_rows(chunks[-1:], jnp.stack(places[-1:]), shape, remainder)
    return (coefficients, remainder)


def solution(mesh):
    in_specs = (P(("row", "col"), None), P(("row", "col")), P())
    out_specs = (P(None, "col"), P("row", "col"))
    return jax.shard_map(steps, mesh=mesh, in_specs=in_specs, out_specs=out_specs, check_vma=False)
```
